32 devices in a mesh: grp: 2 (over y), cls: 8 (over z, x), img: 2 (over core).
Axes of the slice: x: 2, y: 2, z: 4, core: 2. Of those that a mesh axis runs over, the one named last changes fastest.
Arguments:
- embeddings: bfloat16 [4096, 1536], P(('grp', 'img'), 'cls'), parts along dimension 0, may hold values from -6 to 6, as said below
- labels: int32 [4096], P(('grp', 'img')), parts along dimension 0, may hold values from 0 to 1023
- weights: float32 [3072, 1024], P(('grp', 'img'), 'cls'), parts along dimension 0, may hold values from -12 to 12, as said below
- strength: int32 [2], P('grp'), parts along dimension 0, may hold values from 0 to 3
Outputs:
- new_weights: float32 [3072, 1024], P(('grp', 'img'), 'cls'), parts along dimension 0
- losses: float32 [4096], P(('grp', 'img')), parts along dimension 0
The draws below stay inside these ranges and needn't reach their ends.
There are 2 independent parts, one for each index of `grp`. The reference program is written for one: setup_inputs(seed, part) draws one part's arguments, and reference() takes and returns one part's arrays. A program takes and returns all parts, laid end to end along the dimension named above; each array names one. Nothing has to cross between parts.
Inputs may be any that keep to these rules, and one draw needn't show every extreme that they name: embeddings of order one. Initial probe weights of order a few.
All inputs are finite; a program needn't handle non-finite values.
Results may differ from the reference program's by a relative error of at most 0.0032.
Values may be sent and summed in bfloat16 or wider, within the bound.
A program may use at most 64 MiB of HBM per device.

```python
import math
import jax
import jax.numpy as jnp
from jax import lax

D = 1536
ITERS = 2
CLASSES = 1024
IMAGES = 2048


def base_weights(key):
    return 3.0 * jax.random.truncated_normal(jax.random.fold_in(key, 11), -4.0, 4.0, (D, CLASSES), jnp.float32)


def draw_weights(key, part):
    values = base_weights(key)
    return values


def draw_embeddings(key, part):
    inner = jax.random.fold_in(key, 31)
    values = jax.random.truncated_normal(inner, -4.0, 4.0, (IMAGES, D), jnp.float32)
    return values.astype(jnp.bfloat16)


def touch_ends(result, rng, low, high):
    dims = result.shape
    place = [jax.random.randint(jax.random.fold_in(rng, axis), (), 0, dims[axis]) for axis in range(len(dims))]
    result = result.at[tuple(place)].set(low)
    longest = dims.index(max(dims))
    place[longest] = (place[longest] + 1) % dims[longest]
    return result.at[tuple(place)].set(high)


def setup_inputs(seed: int = 0, part: int = 0) -> dict:
    splits = jax.random.split(jax.random.key(seed), 5)
    part_keys = jax.random.split(jax.random.fold_in(splits[4], part), 5)
    return {
        "embeddings": draw_embeddings(jax.random.fold_in(jax.random.fold_in(splits[4], part), 71), part),
        "labels": touch_ends(jax.random.randint(part_keys[1], (IMAGES,), 0, CLASSES), jax.random.fold_in(part_keys[1], 1), 0, CLASSES - 1).astype(jnp.int32),
        "weights": draw_weights(jax.random.fold_in(jax.random.fold_in(splits[4], part), 71), part),
        "strength": jax.random.randint(part_keys[3], (1,), 0, 4).astype(jnp.int32),
    }


def reference(embeddings, labels, weights, strength):
    scale = 1.0 / math.sqrt(D)
    lam = 16.0 * 0.01 * jnp.exp2(strength[0].astype(jnp.float32))
    classes = lax.iota(jnp.int32, CLASSES)
    onehot = (labels[:, None] == classes[None, :]).astype(jnp.float32)
    master = weights
    losses = jnp.zeros((IMAGES,), jnp.float32)
    for step in range(ITERS):
        operand = master.astype(jnp.bfloat16)
        logits = jnp.dot(embeddings, operand, preferred_element_type=jnp.float32) * scale
        top = lax.optimization_barrier(jnp.max(logits, axis=1))
        total = lax.optimization_barrier(jnp.sum(jnp.exp(logits - top[:, None]), axis=1))
        lse = top + jnp.log(total)
        picked = lax.optimization_barrier(jnp.sum(logits * onehot, axis=1))
        losses = lse - picked
        resid = (jnp.exp(logits - lse[:, None]) - onehot).astype(jnp.bfloat16)
        grad = lax.dot_general(embeddings, resid, (((0,), (0,)), ((), ())), preferred_element_type=jnp.float32) * scale
        moved = master - 16.0 * grad
        master = jnp.sign(moved) * jnp.maximum(jnp.abs(moved) - lam, 0.0)
    return (master, losses)
```

```python
import functools
import math

import jax
import jax.numpy as jnp
from jax import lax
from jax.experimental import pallas as pl
from jax.experimental.pallas import tpu as pltpu
from jax.sharding import PartitionSpec as P

D = 1536
ITERS = 2
MESH = pl.DeviceIdType.MESH
SCALE = 1.0 / math.sqrt(D)

NX, NZ = 2, 4
N = NX * NZ
IMGS, WIDTH, CLS = 1024, 192, 128
UP, DOWN, ACROSS = 0, 1, 2
MAIN, TAIL_A, TAIL_B = 0, 1, 2
CHUNK = 256


def shrink(master, grad, lam):
    moved = master - 16.0 * grad
    return jnp.sign(moved) * jnp.maximum(jnp.abs(moved) - lam, 0.0)


def nt(a, b):
    return lax.dot_general(a, b, (((1,), (1,)), ((), ())), preferred_element_type=jnp.float32)


def kernel(x_ref, lab_ref, w_ref, s_ref, out_ref, loss_ref,
           xd, tp, wb, wb2, master, acc, ex, resid, gsend, grecv, lses, picks,
           send_sem, recv_sem, w_send, w_recv, g_send, g_recv, l_send, l_recv):
    me = lax.axis_index("cls")
    img = lax.axis_index("img")
    grp = lax.axis_index("grp")
    z, x = me // NX, me % NX
    mate = (grp, me, 1 - img)

    barrier = pltpu.get_barrier_semaphore()
    for k in range(1, N):
        pl.semaphore_signal(barrier, inc=1, device_id=(grp, (me + k) % N, img), device_id_type=MESH)
    pl.semaphore_signal(barrier, inc=1, device_id=mate, device_id_type=MESH)
    pl.semaphore_wait(barrier, N)

    def main_tile(sz, sx):
        return (sz // 2) * 6 + (sz % 2) * 2 + sx

    def tail_tile(sz):
        return (sz // 2) * 6 + 4 + sz % 2

    def place(sz, sx, q):
        if q == MAIN:
            return xd.at[main_tile(sz, sx)]
        if q == TAIL_A:
            return tp.at[sz * NX + sx, pl.ds(0, 256)]
        return tp.at[sz * NX + sx, pl.ds(256, 256)]

    def copy(sz, sx, q, way, src=None):
        to = {UP: me + NX, DOWN: me - NX, ACROSS: z * NX + 1 - x}[way]
        ref = place(sz, sx, q)
        return pltpu.make_async_remote_copy(
            src_ref=ref if src is None else src,
            dst_ref=ref,
            send_sem=send_sem.at[way, sz * NX + sx, q],
            recv_sem=recv_sem.at[sz * NX + sx, q],
            device_id=(grp, to, img),
            device_id_type=MESH,
        )

    started = []

    def send(cond, *args, **kw):
        @pl.when(cond)
        def _():
            copy(*args, **kw).start()
        started.append((cond, args, kw))

    def arrived(sz, sx, q):
        copy(sz, sx, q, ACROSS).wait_recv()

    yes = z >= 0
    own = dict(src=x_ref.at[:, pl.ds(0, 128)])
    send(yes, z, x, MAIN, ACROSS, **own)
    send(z < NZ - 1, z, x, MAIN, UP, **own)
    send(z > 0, z, x, MAIN, DOWN, **own)
    tp[me] = jnp.concatenate([x_ref[0:512, 128:192], x_ref[512:1024, 128:192]], axis=1)
    for q in (TAIL_B, TAIL_A):
        send(yes, z, x, q, ACROSS)
        send(z < NZ - 1, z, x, q, UP)
        send(z > 0, z, x, q, DOWN)
    xd[main_tile(z, x)] = x_ref[:, 0:128]

    order = [(192 * k, 128) for k in range(4)] + [(192 * k + 128, 64) for k in range(4)]
    rows = jnp.concatenate([w_ref[a:a + n] for a, n in order], axis=0)
    for j in range(3):
        part = rows[256 * j:256 * j + 256].T
        master[j] = part
        wb[img * 3 + j] = part.astype(jnp.bfloat16)

    def weights_copy(buf, step):
        half = buf.at[pl.ds(img * 3, 3)]
        return pltpu.make_async_remote_copy(
            src_ref=half, dst_ref=half, send_sem=w_send.at[step], recv_sem=w_recv.at[step],
            device_id=mate, device_id_type=MESH)

    def weights_arrived(buf, step):
        half = buf.at[pl.ds((1 - img) * 3, 3)]
        pltpu.make_async_remote_copy(
            src_ref=half, dst_ref=half, send_sem=w_send.at[step], recv_sem=w_recv.at[step],
            device_id=mate, device_id_type=MESH).wait_recv()

    weights_copy(wb, 0).start()
    acc[...] = jnp.zeros_like(acc)

    def block(g, r=slice(None)):
        return jnp.concatenate([xd[2 * g, r], xd[2 * g + 1, r]], axis=1)

    def add_group(buf, g):
        for n in range(0, IMGS, CHUNK):
            r = slice(n, n + CHUNK)
            acc[:, r] += nt(buf[g], block(g, r))

    def finish(sz):
        arrived(sz, 1 - x, MAIN)
        add_group(wb, (sz // 2) * 3 + sz % 2)

    def tails(sz):
        lo, hi = tp[sz * NX], tp[sz * NX + 1]
        t = tail_tile(sz)
        xd[t, 0:512] = jnp.concatenate([lo[:, :64], hi[:, :64]], axis=1)
        xd[t, 512:1024] = jnp.concatenate([lo[:, 64:], hi[:, 64:]], axis=1)

    arrived(z, 1 - x, TAIL_B)
    send(z < NZ - 1, z, 1 - x, TAIL_B, UP)
    send(z > 0, z, 1 - x, TAIL_B, DOWN)

    for d in range(NZ):
        if d > 0:
            for sz, here, way, onward in (
                (z - d, z >= d, UP, z < NZ - 1),
                (z + d, z + d < NZ, DOWN, z > 0),
            ):
                @pl.when(here)
                def _(sz=sz):
                    arrived(sz, x, MAIN)
                both = jnp.logical_and(here, onward)
                send(both, sz, x, MAIN, way)
                send(here, sz, x, MAIN, ACROSS)
            for sz, here, way, onward in (
                (z - d, z >= d, UP, z < NZ - 1),
                (z + d, z + d < NZ, DOWN, z > 0),
            ):
                both = jnp.logical_and(here, onward)
                for sx, q in ((x, TAIL_B), (x, TAIL_A), (1 - x, TAIL_B)):
                    @pl.when(here)
                    def _(sz=sz, sx=sx, q=q):
                        arrived(sz, sx, q)
                    send(both, sz, sx, q, way)
                send(here, sz, x, TAIL_A, ACROSS)
        if d == 0:
            pass
        elif d == 1:
            weights_arrived(wb, 0)
            finish(z)
        else:
            for sz, here in ((z - d + 1, z >= d - 1), (z + d - 1, z + d - 1 < NZ)):
                @pl.when(here)
                def _(sz=sz):
                    finish(sz)
    for sz, here in ((z - NZ + 1, z >= NZ - 1), (z + NZ - 1, z == 0)):
        @pl.when(here)
        def _(sz=sz):
            finish(sz)
    for sz in range(NZ):
        arrived(sz, 1 - x, TAIL_A)
    for sz in range(NZ):
        tails(sz)
    for h in range(2):
        add_group(wb, h * 3 + 2)

    lam = 0.16 * jnp.exp2(s_ref[...].astype(jnp.float32))
    first = me * CLS

    def stat_copy(buf, sems, step, k):
        return pltpu.make_async_remote_copy(
            src_ref=buf.at[me], dst_ref=buf.at[me],
            send_sem=l_send.at[sems, k], recv_sem=l_recv.at[sems, me],
            device_id=(grp, (me + k) % N, img), device_id_type=MESH)

    def stat_arrived(buf, sems, k):
        frm = (me + k) % N
        pltpu.make_async_remote_copy(
            src_ref=buf.at[frm], dst_ref=buf.at[frm],
            send_sem=l_send.at[sems, k], recv_sem=l_recv.at[sems, frm],
            device_id=(grp, frm, img), device_id_type=MESH).wait_recv()

    def grad_copy(step, j):
        return pltpu.make_async_remote_copy(
            src_ref=gsend.at[step, j], dst_ref=grecv.at[step, j],
            send_sem=g_send.at[step, j], recv_sem=g_recv.at[step, j],
            device_id=mate, device_id_type=MESH)

    for step in range(ITERS):
        last = step == ITERS - 1
        tops = []
        lse_buf = lses.at[step]
        for n in range(0, IMGS, CHUNK):
            r = slice(n, n + CHUNK)
            logits = acc[:, r] * SCALE
            top = jnp.max(logits, axis=0, keepdims=True)
            e = jnp.exp(logits - top)
            ex[:, r] = e
            lse_buf[me, :, r] = top + jnp.log(jnp.sum(e, axis=0, keepdims=True))
            tops.append(top)
            if last:
                hot = lab_ref[:, r] == first + lax.broadcasted_iota(jnp.int32, (CLS, CHUNK), 0)
                picks[me, :, r] = jnp.sum(jnp.where(hot, logits, 0.0), axis=0, keepdims=True)
        for k in range(1, N):
            stat_copy(lse_buf, step, step, k).start()
        if last:
            for k in range(1, N):
                stat_copy(picks, 2, step, k).start()
        for k in range(1, N):
            stat_arrived(lse_buf, step, k)
        for n in range(0, IMGS, CHUNK):
            r = slice(n, n + CHUNK)
            parts = [lse_buf[k, :, r] for k in range(N)]
            top = functools.reduce(jnp.maximum, parts)
            lse = top + jnp.log(sum(jnp.exp(p - top) for p in parts))
            if last:
                loss_ref[:, r] = lse
            hot = lab_ref[:, r] == first + lax.broadcasted_iota(jnp.int32, (CLS, CHUNK), 0)
            prob = ex[:, r] * jnp.exp(tops[n // CHUNK] - lse)
            resid[:, r] = (prob - jnp.where(hot, 1.0, 0.0)).astype(jnp.bfloat16)
        for j in range(3):
            gsend[step, j] = jnp.dot(
                resid[...], block((1 - img) * 3 + j), preferred_element_type=jnp.float32)
            grad_copy(step, j).start()
        for j in range(3):
            grad = jnp.dot(resid[...], block(img * 3 + j), preferred_element_type=jnp.float32)
            grad_copy(step, j).wait_recv()
            moved = master[j] - 16.0 * ((grad + grecv[step, j]) * SCALE)
            new = moved - jnp.clip(moved, -lam, lam)
            master[j] = new
            if not last:
                wb2[img * 3 + j] = new.astype(jnp.bfloat16)
        if not last:
            weights_copy(wb2, 1).start()
            acc[...] = jnp.zeros_like(acc)
            for j in range(3):
                add_group(wb2, img * 3 + j)
            weights_arrived(wb2, 1)
            for j in range(3):
                add_group(wb2, (1 - img) * 3 + j)

    at = 0
    new_rows = jnp.concatenate([master[j].T for j in range(3)], axis=0)
    for a, n in order:
        out_ref[a:a + n] = new_rows[at:at + n]
        at += n
    for k in range(1, N):
        stat_arrived(picks, 2, k)
    loss_ref[...] = loss_ref[...] - sum(picks[k] for k in range(N))

    for cond, args, kw in started:
        @pl.when(cond)
        def _(args=args, kw=kw):
            copy(*args, **kw).wait_send()
    weights_copy(wb, 0).wait_send()
    weights_copy(wb2, 1).wait_send()
    for step in range(ITERS):
        for j in range(3):
            grad_copy(step, j).wait_send()
        for k in range(1, N):
            stat_copy(lses.at[step], step, step, k).wait_send()
    for k in range(1, N):
        stat_copy(picks, 2, 1, k).wait_send()


def fused(embeddings, labels, weights, strength):
    vmem = pl.BlockSpec(memory_space=pltpu.VMEM)
    f32, bf16 = jnp.float32, jnp.bfloat16
    new_weights, losses = pl.pallas_call(
        kernel,
        out_shape=(
            jax.ShapeDtypeStruct((768, CLS), f32),
            jax.ShapeDtypeStruct((1, IMGS), f32),
        ),
        in_specs=[vmem] * 4,
        out_specs=(vmem, vmem),
        scratch_shapes=[
            pltpu.VMEM((12, IMGS, 128), bf16),
            pltpu.VMEM((N, 512, 128), bf16),
            pltpu.VMEM((6, CLS, 256), bf16),
            pltpu.VMEM((6, CLS, 256), bf16),
            pltpu.VMEM((3, CLS, 256), f32),
            pltpu.VMEM((CLS, IMGS), f32),
            pltpu.VMEM((CLS, IMGS), f32),
            pltpu.VMEM((CLS, IMGS), bf16),
            pltpu.VMEM((ITERS, 3, CLS, 256), f32),
            pltpu.VMEM((ITERS, 3, CLS, 256), f32),
            pltpu.VMEM((ITERS, N, 1, IMGS), f32),
            pltpu.VMEM((N, 1, IMGS), f32),
            pltpu.SemaphoreType.DMA((3, N, 3)),
            pltpu.SemaphoreType.DMA((N, 3)),
            pltpu.SemaphoreType.DMA((2,)),
            pltpu.SemaphoreType.DMA((2,)),
            pltpu.SemaphoreType.DMA((2, 3)),
            pltpu.SemaphoreType.DMA((2, 3)),
            pltpu.SemaphoreType.DMA((3, N)),
            pltpu.SemaphoreType.DMA((3, N)),
        ],
        compiler_params=pltpu.CompilerParams(
            collective_id=0, has_side_effects=True, vmem_limit_bytes=40 * 1024 * 1024
        ),
    )(embeddings, labels.reshape(1, IMGS), weights, strength.reshape(1, 1))
    return new_weights, losses.reshape(IMGS)


def general(embeddings, labels, weights, strength):
    lam = 16.0 * 0.01 * jnp.exp2(strength[0].astype(jnp.float32))
    full_x = lax.all_gather(embeddings, "cls", axis=1, tiled=True)
    cls_width = weights.shape[1]
    first_class = lax.axis_index("cls") * cls_width
    classes = first_class + lax.iota(jnp.int32, cls_width)
    onehot = (labels[:, None] == classes[None, :]).astype(jnp.float32)
    master = lax.all_gather(weights, "img", axis=0, tiled=True)
    operand = master.astype(jnp.bfloat16)
    losses = jnp.zeros((labels.shape[0],), jnp.float32)
    for step in range(ITERS):
        logits = jnp.dot(full_x, operand, preferred_element_type=jnp.float32) * SCALE
        local_top = jnp.max(logits, axis=1)
        label_term = jnp.sum(logits * onehot, axis=1)
        top = lax.pmax(local_top, "cls")
        total, picked = lax.psum(
            (jnp.sum(jnp.exp(logits - top[:, None]), axis=1), label_term), "cls"
        )
        lse = top + jnp.log(total)
        losses = lse - picked
        resid = (jnp.exp(logits - lse[:, None]) - onehot).astype(jnp.bfloat16)
        grad_local = (
            lax.dot_general(
                full_x, resid, (((0,), (0,)), ((), ())), preferred_element_type=jnp.float32
            )
            * SCALE
        )
        grad = lax.psum(grad_local, "img")
        master = shrink(master, grad, lam)
        operand = master.astype(jnp.bfloat16)
    rows = weights.shape[0]
    new_weights = lax.dynamic_slice_in_dim(master, lax.axis_index("img") * rows, rows, 0)
    return (new_weights, losses)


def solution(mesh):
    placed = (P(("grp", "img"), "cls"), P(("grp", "img")), P(("grp", "img"), "cls"), P("grp"))
    return jax.shard_map(
        fused if mesh.shape["cls"] == N else general,
        mesh=mesh,
        in_specs=placed,
        out_specs=(P(("grp", "img"), "cls"), P(("grp", "img"))),
        check_vma=False,
    )
```

```python
import functools
import math

import jax
import jax.numpy as jnp
from jax import lax
from jax.experimental import pallas as pl
from jax.experimental.pallas import tpu as pltpu
from jax.sharding import PartitionSpec as P

D = 1536
ITERS = 2
MESH = pl.DeviceIdType.MESH
SCALE = 1.0 / math.sqrt(D)

NX, NZ = 2, 4
N = NX * NZ
IMGS, WIDTH, CLS = 1024, 192, 128
UP, DOWN, ACROSS = 0, 1, 2
PARTS = ((0, 96), (96, 64), (160, 32))
LAST = len(PARTS) - 1
CHUNK = 256


def shrink(master, grad, lam):
    moved = master - 16.0 * grad
    return jnp.sign(moved) * jnp.maximum(jnp.abs(moved) - lam, 0.0)


def kernel(x_hbm, lab_ref, w_hbm, s_ref, out_ref, loss_ref,
           w_ref, load, xd, wb, wb2, acc, ex, resid, gsend, grecv, lses, picks,
           send_sem, recv_sem, w_send, w_recv, g_send, g_recv, l_send, l_recv):
    me = lax.axis_index("cls")
    img = lax.axis_index("img")
    grp = lax.axis_index("grp")
    z, x = me // NX, me % NX
    mate = (grp, me, 1 - img)
    has_up, has_down = z < NZ - 1, z > 0
    yes = z >= 0

    def rows(at, n):
        return pl.ds(pl.multiple_of(at, 16), n)

    loads = [
        pltpu.make_async_copy(x_hbm, xd.at[rows(me * WIDTH, WIDTH)], load.at[0]),
        pltpu.make_async_copy(w_hbm, w_ref, load.at[1]),
    ]
    for c in loads:
        c.start()
    barrier = pltpu.get_barrier_semaphore()
    pl.semaphore_signal(barrier, inc=1, device_id=mate, device_id_type=MESH)
    pl.semaphore_signal(
        barrier, inc=1, device_id=(grp, z * NX + 1 - x, img), device_id_type=MESH)

    @pl.when(has_up)
    def _():
        pl.semaphore_signal(barrier, inc=1, device_id=(grp, me + NX, img), device_id_type=MESH)

    @pl.when(has_down)
    def _():
        pl.semaphore_signal(barrier, inc=1, device_id=(grp, me - NX, img), device_id_type=MESH)

    def place(sz, sx, q):
        at, n = PARTS[q]
        return xd.at[rows((sz * NX + sx) * WIDTH + at, n)]

    def copy(sz, sx, q, way):
        to = {UP: me + NX, DOWN: me - NX, ACROSS: z * NX + 1 - x}[way]
        ref = place(sz, sx, q)
        return pltpu.make_async_remote_copy(
            src_ref=ref,
            dst_ref=ref,
            send_sem=send_sem.at[way, sz * NX + sx, q],
            recv_sem=recv_sem.at[sz * NX + sx, q],
            device_id=(grp, to, img),
            device_id_type=MESH,
        )

    started = []

    def send(cond, *args):
        @pl.when(cond)
        def _():
            copy(*args).start()
        started.append((cond, args))

    def arrived(sz, sx, q):
        copy(sz, sx, q, ACROSS).wait_recv()

    def put_weights(buf, values):
        for j in range(2):
            buf[img * 2 + j] = values[384 * j:384 * j + 384].T.astype(jnp.bfloat16)

    loads[1].wait()
    put_weights(wb, w_ref[...])
    acc[...] = jnp.zeros_like(acc)
    loads[0].wait()
    pl.semaphore_wait(barrier, 2 + has_up.astype(jnp.int32) + has_down.astype(jnp.int32))
    send(yes, z, x, LAST, ACROSS)
    for q in range(LAST):
        send(has_up, z, x, q, UP)
        send(has_down, z, x, q, DOWN)
        send(yes, z, x, q, ACROSS)

    def weights_copy(buf, step):
        half = buf.at[pl.ds(img * 2, 2)]
        return pltpu.make_async_remote_copy(
            src_ref=half, dst_ref=half, send_sem=w_send.at[step], recv_sem=w_recv.at[step],
            device_id=mate, device_id_type=MESH)

    def weights_arrived(buf, step):
        half = buf.at[pl.ds((1 - img) * 2, 2)]
        pltpu.make_async_remote_copy(
            src_ref=half, dst_ref=half, send_sem=w_send.at[step], recv_sem=w_recv.at[step],
            device_id=mate, device_id_type=MESH).wait_recv()

    weights_copy(wb, 0).start()

    def add_group(sz):
        for n in range(0, IMGS, CHUNK):
            r = slice(n, n + CHUNK)
            acc[:, r] += jnp.dot(
                wb[sz], xd[rows(sz * 384, 384), r], preferred_element_type=jnp.float32)

    def half_logits(h, r):
        w = jnp.concatenate([wb2[2 * h], wb2[2 * h + 1]], axis=1)
        return jnp.dot(w, xd[rows(h * 768, 768), r], preferred_element_type=jnp.float32)

    def finish(sz):
        for q in range(LAST):
            arrived(sz, 1 - x, q)
        add_group(sz)

    def sides(d):
        return (
            (z - d, z >= d, UP, has_up),
            (z + d, z + d < NZ, DOWN, has_down),
        )

    for d in range(NZ):
        if d > 0:
            for q in range(LAST):
                for sz, here, way, onward in sides(d):
                    @pl.when(here)
                    def _(sz=sz, q=q):
                        arrived(sz, x, q)
                    send(jnp.logical_and(here, onward), sz, x, q, way)
                    send(here, sz, x, q, ACROSS)
        else:
            arrived(z, 1 - x, LAST)
        for sx in (x, 1 - x):
            send(jnp.logical_and(z == d, has_up), z, sx, LAST, UP)
            send(jnp.logical_and(NZ - 1 - z == d, has_down), z, sx, LAST, DOWN)
        if d == 1:
            weights_arrived(wb, 0)
            finish(z)
    for d in range(1, NZ):
        for sz, here, way, onward in sides(d):
            for sx in (x, 1 - x):
                @pl.when(here)
                def _(sz=sz, sx=sx):
                    arrived(sz, sx, LAST)
                send(jnp.logical_and(here, onward), sz, sx, LAST, way)
        for sz, here, _, _ in sides(d - 1) if d > 1 else ():
            @pl.when(here)
            def _(sz=sz):
                finish(sz)

    for sz, here, _, _ in sides(NZ - 1):
        @pl.when(here)
        def _(sz=sz):
            finish(sz)

    lam = 0.16 * jnp.exp2(s_ref[...].astype(jnp.float32))
    first = me * CLS

    def stat_copy(buf, sems, k):
        return pltpu.make_async_remote_copy(
            src_ref=buf.at[me], dst_ref=buf.at[me],
            send_sem=l_send.at[sems, k], recv_sem=l_recv.at[sems, me],
            device_id=(grp, (me + k) % N, img), device_id_type=MESH)

    def stat_arrived(buf, sems, k):
        frm = (me + k) % N
        pltpu.make_async_remote_copy(
            src_ref=buf.at[frm], dst_ref=buf.at[frm],
            send_sem=l_send.at[sems, k], recv_sem=l_recv.at[sems, frm],
            device_id=(grp, frm, img), device_id_type=MESH).wait_recv()

    def grad_copy(step, j):
        return pltpu.make_async_remote_copy(
            src_ref=gsend.at[step, j], dst_ref=grecv.at[step, j],
            send_sem=g_send.at[step, j], recv_sem=g_recv.at[step, j],
            device_id=mate, device_id_type=MESH)

    def grad_part(h, j):
        return lax.dot_general(
            xd[rows(h * 768 + j * 256, 256), :], resid[...], (((1,), (1,)), ((), ())),
            preferred_element_type=jnp.float32)

    for step in range(ITERS):
        last = step == ITERS - 1
        tops = []
        lse_buf = lses.at[step]
        if step > 0:
            weights_arrived(wb2, 1)
        for n in range(0, IMGS, CHUNK):
            r = slice(n, n + CHUNK)
            logits = acc[:, r] * SCALE
            if step > 0:
                logits = (acc[:, r] + half_logits(1 - img, r)) * SCALE
            top = jnp.max(logits, axis=0, keepdims=True)
            e = jnp.exp(logits - top)
            ex[:, r] = e
            lse_buf[me, :, r] = top + jnp.log(jnp.sum(e, axis=0, keepdims=True))
            tops.append(top)
            if last:
                hot = lab_ref[:, r] == first + lax.broadcasted_iota(jnp.int32, (CLS, CHUNK), 0)
                picks[me, :, r] = jnp.sum(jnp.where(hot, logits, 0.0), axis=0, keepdims=True)
        for k in range(1, N):
            stat_copy(lse_buf, step, k).start()
        if last:
            for k in range(1, N):
                stat_copy(picks, 2, k).start()
        for k in range(1, N):
            stat_arrived(lse_buf, step, k)
        for n in range(0, IMGS, CHUNK):
            r = slice(n, n + CHUNK)
            parts = [lse_buf[k, :, r] for k in range(N)]
            top = functools.reduce(jnp.maximum, parts)
            lse = top + jnp.log(sum(jnp.exp(p - top) for p in parts))
            if last:
                loss_ref[:, r] = lse
            hot = lab_ref[:, r] == first + lax.broadcasted_iota(jnp.int32, (CLS, CHUNK), 0)
            prob = ex[:, r] * jnp.exp(tops[n // CHUNK] - lse)
            resid[:, r] = (prob - jnp.where(hot, 1.0, 0.0)).astype(jnp.bfloat16)
        for j in range(3):
            gsend[step, j] = grad_part(1 - img, j)
            grad_copy(step, j).start()
        for j in range(3):
            r = slice(256 * j, 256 * j + 256)
            grad = grad_part(img, j)
            grad_copy(step, j).wait_recv()
            moved = w_ref[r] - 16.0 * ((grad + grecv[step, j]) * SCALE)
            new = moved - jnp.clip(moved, -lam, lam)
            if last:
                out_ref[r] = new
            else:
                w_ref[r] = new
        if not last:
            put_weights(wb2, w_ref[...])
            weights_copy(wb2, 1).start()
            for n in range(0, IMGS, CHUNK):
                acc[:, n:n + CHUNK] = half_logits(img, slice(n, n + CHUNK))

    for k in range(1, N):
        stat_arrived(picks, 2, k)
    loss_ref[...] = loss_ref[...] - sum(picks[k] for k in range(N))

    for cond, args in started:
        @pl.when(cond)
        def _(args=args):
            copy(*args).wait_send()
    weights_copy(wb, 0).wait_send()
    weights_copy(wb2, 1).wait_send()
    for step in range(ITERS):
        for j in range(3):
            grad_copy(step, j).wait_send()
        for k in range(1, N):
            stat_copy(lses.at[step], step, k).wait_send()
    for k in range(1, N):
        stat_copy(picks, 2, k).wait_send()


def fused(embeddings, labels, weights, strength):
    vmem = pl.BlockSpec(memory_space=pltpu.VMEM)
    hbm = pl.BlockSpec(memory_space=pl.ANY)
    f32, bf16 = jnp.float32, jnp.bfloat16
    new_weights, losses = pl.pallas_call(
        kernel,
        out_shape=(
            jax.ShapeDtypeStruct((768, CLS), f32),
            jax.ShapeDtypeStruct((1, IMGS), f32),
        ),
        in_specs=[hbm, vmem, hbm, vmem],
        out_specs=(vmem, vmem),
        scratch_shapes=[
            pltpu.VMEM((768, CLS), f32),
            pltpu.SemaphoreType.DMA((2,)),
            pltpu.VMEM((D, IMGS), bf16),
            pltpu.VMEM((4, CLS, 384), bf16),
            pltpu.VMEM((4, CLS, 384), bf16),
            pltpu.VMEM((CLS, IMGS), f32),
            pltpu.VMEM((CLS, IMGS), f32),
            pltpu.VMEM((CLS, IMGS), bf16),
            pltpu.VMEM((ITERS, 3, 256, CLS), f32),
            pltpu.VMEM((ITERS, 3, 256, CLS), f32),
            pltpu.VMEM((ITERS, N, 1, IMGS), f32),
            pltpu.VMEM((N, 1, IMGS), f32),
            pltpu.SemaphoreType.DMA((3, N, len(PARTS))),
            pltpu.SemaphoreType.DMA((N, len(PARTS))),
            pltpu.SemaphoreType.DMA((2,)),
            pltpu.SemaphoreType.DMA((2,)),
            pltpu.SemaphoreType.DMA((2, 3)),
            pltpu.SemaphoreType.DMA((2, 3)),
            pltpu.SemaphoreType.DMA((3, N)),
            pltpu.SemaphoreType.DMA((3, N)),
        ],
        compiler_params=pltpu.CompilerParams(
            collective_id=0, has_side_effects=True, vmem_limit_bytes=60 * 1024 * 1024
        ),
    )(embeddings.T, labels.reshape(1, IMGS), weights, strength.reshape(1, 1))
    return new_weights, losses.reshape(IMGS)


def general(embeddings, labels, weights, strength):
    lam = 16.0 * 0.01 * jnp.exp2(strength[0].astype(jnp.float32))
    full_x = lax.all_gather(embeddings, "cls", axis=1, tiled=True)
    cls_width = weights.shape[1]
    first_class = lax.axis_index("cls") * cls_width
    classes = first_class + lax.iota(jnp.int32, cls_width)
    onehot = (labels[:, None] == classes[None, :]).astype(jnp.float32)
    master = lax.all_gather(weights, "img", axis=0, tiled=True)
    operand = master.astype(jnp.bfloat16)
    losses = jnp.zeros((labels.shape[0],), jnp.float32)
    for step in range(ITERS):
        logits = jnp.dot(full_x, operand, preferred_element_type=jnp.float32) * SCALE
        local_top = jnp.max(logits, axis=1)
        label_term = jnp.sum(logits * onehot, axis=1)
        top = lax.pmax(local_top, "cls")
        total, picked = lax.psum(
            (jnp.sum(jnp.exp(logits - top[:, None]), axis=1), label_term), "cls"
        )
        lse = top + jnp.log(total)
        losses = lse - picked
        resid = (jnp.exp(logits - lse[:, None]) - onehot).astype(jnp.bfloat16)
        grad_local = (
            lax.dot_general(
                full_x, resid, (((0,), (0,)), ((), ())), preferred_element_type=jnp.float32
            )
            * SCALE
        )
        grad = lax.psum(grad_local, "img")
        master = shrink(master, grad, lam)
        operand = master.astype(jnp.bfloat16)
    rows = weights.shape[0]
    new_weights = lax.dynamic_slice_in_dim(master, lax.axis_index("img") * rows, rows, 0)
    return (new_weights, losses)


def solution(mesh):
    placed = (P(("grp", "img"), "cls"), P(("grp", "img")), P(("grp", "img"), "cls"), P("grp"))
    return jax.shard_map(
        fused if mesh.shape["cls"] == N else general,
        mesh=mesh,
        in_specs=placed,
        out_specs=(P(("grp", "img"), "cls"), P(("grp", "img"))),
        check_vma=False,
    )
```

```python
import functools
import math

import jax
import jax.numpy as jnp
from jax import lax
from jax.experimental import pallas as pl
from jax.experimental.pallas import tpu as pltpu
from jax.sharding import PartitionSpec as P

D = 1536
ITERS = 2
MESH = pl.DeviceIdType.MESH
SCALE = 1.0 / math.sqrt(D)

NX, NZ = 2, 4
N = NX * NZ
IMGS, WIDTH, CLS = 1024, 192, 128
UP, DOWN, ACROSS = 0, 1, 2
PARTS = ((0, 96), (96, 64), (160, 32))
LAST = len(PARTS) - 1
CHUNK = 256


def shrink(master, grad, lam):
    moved = master - 16.0 * grad
    return jnp.sign(moved) * jnp.maximum(jnp.abs(moved) - lam, 0.0)


def kernel(x_hbm, lab_ref, w_hbm, s_ref, out_ref, loss_ref,
           w_ref, load, xd, wb, wb2, acc, ex, resid, gsend, grecv, lses, picks,
           send_sem, recv_sem, w_send, w_recv, g_send, g_recv, l_send, l_recv):
    me = lax.axis_index("cls")
    img = lax.axis_index("img")
    grp = lax.axis_index("grp")
    z, x = me // NX, me % NX
    mate = (grp, me, 1 - img)
    has_up, has_down = z < NZ - 1, z > 0
    yes = z >= 0

    def rows(at, n):
        return pl.ds(pl.multiple_of(at, 16), n)

    loads = [
        pltpu.make_async_copy(x_hbm, xd.at[rows(me * WIDTH, WIDTH)], load.at[0]),
        pltpu.make_async_copy(w_hbm, w_ref, load.at[1]),
    ]
    for c in loads:
        c.start()
    barrier = pltpu.get_barrier_semaphore()
    pl.semaphore_signal(barrier, inc=1, device_id=mate, device_id_type=MESH)
    pl.semaphore_signal(
        barrier, inc=1, device_id=(grp, z * NX + 1 - x, img), device_id_type=MESH)

    @pl.when(has_up)
    def _():
        pl.semaphore_signal(barrier, inc=1, device_id=(grp, me + NX, img), device_id_type=MESH)

    @pl.when(has_down)
    def _():
        pl.semaphore_signal(barrier, inc=1, device_id=(grp, me - NX, img), device_id_type=MESH)

    def place(sz, sx, q):
        at, n = PARTS[q]
        return xd.at[rows((sz * NX + sx) * WIDTH + at, n)]

    def copy(sz, sx, q, way):
        to = {UP: me + NX, DOWN: me - NX, ACROSS: z * NX + 1 - x}[way]
        ref = place(sz, sx, q)
        return pltpu.make_async_remote_copy(
            src_ref=ref,
            dst_ref=ref,
            send_sem=send_sem.at[way, sz * NX + sx, q],
            recv_sem=recv_sem.at[sz * NX + sx, q],
            device_id=(grp, to, img),
            device_id_type=MESH,
        )

    started = []

    def send(cond, *args):
        @pl.when(cond)
        def _():
            copy(*args).start()
        started.append((cond, args))

    def arrived(sz, sx, q):
        copy(sz, sx, q, ACROSS).wait_recv()

    def put_weights(buf, values):
        for j in range(2):
            buf[img * 2 + j] = values[384 * j:384 * j + 384].T.astype(jnp.bfloat16)

    loads[1].wait()
    put_weights(wb, w_ref[...])
    acc[...] = jnp.zeros_like(acc)
    loads[0].wait()
    pl.semaphore_wait(barrier, 2 + has_up.astype(jnp.int32) + has_down.astype(jnp.int32))
    send(yes, z, x, LAST, ACROSS)
    for q in range(LAST):
        send(has_up, z, x, q, UP)
        send(has_down, z, x, q, DOWN)
        send(yes, z, x, q, ACROSS)

    def weights_copy(buf, step):
        half = buf.at[pl.ds(img * 2, 2)]
        return pltpu.make_async_remote_copy(
            src_ref=half, dst_ref=half, send_sem=w_send.at[step], recv_sem=w_recv.at[step],
            device_id=mate, device_id_type=MESH)

    def weights_arrived(buf, step):
        half = buf.at[pl.ds((1 - img) * 2, 2)]
        pltpu.make_async_remote_copy(
            src_ref=half, dst_ref=half, send_sem=w_send.at[step], recv_sem=w_recv.at[step],
            device_id=mate, device_id_type=MESH).wait_recv()

    weights_copy(wb, 0).start()

    def add_group(sz):
        for n in range(0, IMGS, CHUNK):
            r = slice(n, n + CHUNK)
            acc[:, r] += jnp.dot(
                wb[sz], xd[rows(sz * 384, 384), r], preferred_element_type=jnp.float32)

    def half_logits(h, r):
        w = jnp.concatenate([wb2[2 * h], wb2[2 * h + 1]], axis=1)
        return jnp.dot(w, xd[rows(h * 768, 768), r], preferred_element_type=jnp.float32)

    def finish(sz):
        for q in range(LAST):
            arrived(sz, 1 - x, q)
        add_group(sz)

    def sides(d):
        return (
            (z - d, z >= d, UP, has_up),
            (z + d, z + d < NZ, DOWN, has_down),
        )

    for d in range(NZ):
        if d > 0:
            for q in range(LAST):
                for sz, here, way, onward in sides(d):
                    @pl.when(here)
                    def _(sz=sz, q=q):
                        arrived(sz, x, q)
                    send(jnp.logical_and(here, onward), sz, x, q, way)
                    send(here, sz, x, q, ACROSS)
        else:
            arrived(z, 1 - x, LAST)
        for sx in (x, 1 - x):
            send(jnp.logical_and(z == d, has_up), z, sx, LAST, UP)
            send(jnp.logical_and(NZ - 1 - z == d, has_down), z, sx, LAST, DOWN)
        if d == 1:
            weights_arrived(wb, 0)
            finish(z)
    for d in range(1, NZ):
        for sz, here, way, onward in sides(d):
            for sx in (x, 1 - x):
                @pl.when(here)
                def _(sz=sz, sx=sx):
                    arrived(sz, sx, LAST)
                send(jnp.logical_and(here, onward), sz, sx, LAST, way)
        for sz, here, _, _ in sides(d - 1) if d > 1 else ():
            @pl.when(here)
            def _(sz=sz):
                finish(sz)

    for sz, here, _, _ in sides(NZ - 1):
        @pl.when(here)
        def _(sz=sz):
            finish(sz)

    lam = 0.16 * jnp.exp2(s_ref[...].astype(jnp.float32))
    first = me * CLS

    def stat_copy(buf, sems, k):
        return pltpu.make_async_remote_copy(
            src_ref=buf.at[me], dst_ref=buf.at[me],
            send_sem=l_send.at[sems, k], recv_sem=l_recv.at[sems, me],
            device_id=(grp, (me + k) % N, img), device_id_type=MESH)

    def stat_arrived(buf, sems, k):
        frm = (me + k) % N
        pltpu.make_async_remote_copy(
            src_ref=buf.at[frm], dst_ref=buf.at[frm],
            send_sem=l_send.at[sems, k], recv_sem=l_recv.at[sems, frm],
            device_id=(grp, frm, img), device_id_type=MESH).wait_recv()

    def grad_copy(step, j):
        return pltpu.make_async_remote_copy(
            src_ref=gsend.at[step, j], dst_ref=grecv.at[step, j],
            send_sem=g_send.at[step, j], recv_sem=g_recv.at[step, j],
            device_id=mate, device_id_type=MESH)

    def grad_part(h, j):
        return lax.dot_general(
            xd[rows(h * 768 + j * 256, 256), :], resid[...], (((1,), (1,)), ((), ())),
            preferred_element_type=jnp.float32)

    for step in range(ITERS):
        last = step == ITERS - 1
        tops = []
        lse_buf = (lses, picks)[step]
        if step > 0:
            weights_arrived(wb2, 1)
        for n in range(0, IMGS, CHUNK):
            r = slice(n, n + CHUNK)
            logits = acc[:, r] * SCALE
            if step > 0:
                logits = (acc[:, r] + half_logits(1 - img, r)) * SCALE
            top = jnp.max(logits, axis=0, keepdims=True)
            e = jnp.exp(logits - top)
            ex[:, r] = e
            lse_buf[me, 0:1, r] = top + jnp.log(jnp.sum(e, axis=0, keepdims=True))
            tops.append(top)
            if last:
                hot = lab_ref[:, r] == first + lax.broadcasted_iota(jnp.int32, (CLS, CHUNK), 0)
                picks[me, 1:2, r] = jnp.sum(jnp.where(hot, logits, 0.0), axis=0, keepdims=True)
        for k in range(1, N):
            stat_copy(lse_buf, step, k).start()
        for k in range(1, N):
            stat_arrived(lse_buf, step, k)
        for n in range(0, IMGS, CHUNK):
            r = slice(n, n + CHUNK)
            parts = [lse_buf[k, 0:1, r] for k in range(N)]
            top = functools.reduce(jnp.maximum, parts)
            lse = top + jnp.log(sum(jnp.exp(p - top) for p in parts))
            if last:
                loss_ref[:, r] = lse - sum(picks[k, 1:2, r] for k in range(N))
            hot = lab_ref[:, r] == first + lax.broadcasted_iota(jnp.int32, (CLS, CHUNK), 0)
            prob = ex[:, r] * jnp.exp(tops[n // CHUNK] - lse)
            resid[:, r] = (prob - jnp.where(hot, 1.0, 0.0)).astype(jnp.bfloat16)
        for j in range(3):
            gsend[step, j] = grad_part(1 - img, j)
            grad_copy(step, j).start()
        for j in range(3):
            r = slice(256 * j, 256 * j + 256)
            grad = grad_part(img, j)
            grad_copy(step, j).wait_recv()
            moved = w_ref[r] - 16.0 * ((grad + grecv[step, j]) * SCALE)
            new = moved - jnp.clip(moved, -lam, lam)
            if last:
                out_ref[r] = new
            else:
                w_ref[r] = new
        if not last:
            put_weights(wb2, w_ref[...])
            weights_copy(wb2, 1).start()
            for n in range(0, IMGS, CHUNK):
                acc[:, n:n + CHUNK] = half_logits(img, slice(n, n + CHUNK))

    for cond, args in started:
        @pl.when(cond)
        def _(args=args):
            copy(*args).wait_send()
    weights_copy(wb, 0).wait_send()
    weights_copy(wb2, 1).wait_send()
    for step in range(ITERS):
        for j in range(3):
            grad_copy(step, j).wait_send()
        for k in range(1, N):
            stat_copy((lses, picks)[step], step, k).wait_send()


def fused(embeddings, labels, weights, strength):
    vmem = pl.BlockSpec(memory_space=pltpu.VMEM)
    hbm = pl.BlockSpec(memory_space=pl.ANY)
    f32, bf16 = jnp.float32, jnp.bfloat16
    new_weights, losses = pl.pallas_call(
        kernel,
        out_shape=(
            jax.ShapeDtypeStruct((768, CLS), f32),
            jax.ShapeDtypeStruct((1, IMGS), f32),
        ),
        in_specs=[hbm, vmem, hbm, vmem],
        out_specs=(vmem, vmem),
        scratch_shapes=[
            pltpu.VMEM((768, CLS), f32),
            pltpu.SemaphoreType.DMA((2,)),
            pltpu.VMEM((D, IMGS), bf16),
            pltpu.VMEM((4, CLS, 384), bf16),
            pltpu.VMEM((4, CLS, 384), bf16),
            pltpu.VMEM((CLS, IMGS), f32),
            pltpu.VMEM((CLS, IMGS), f32),
            pltpu.VMEM((CLS, IMGS), bf16),
            pltpu.VMEM((ITERS, 3, 256, CLS), f32),
            pltpu.VMEM((ITERS, 3, 256, CLS), f32),
            pltpu.VMEM((N, 1, IMGS), f32),
            pltpu.VMEM((N, 2, IMGS), f32),
            pltpu.SemaphoreType.DMA((3, N, len(PARTS))),
            pltpu.SemaphoreType.DMA((N, len(PARTS))),
            pltpu.SemaphoreType.DMA((2,)),
            pltpu.SemaphoreType.DMA((2,)),
            pltpu.SemaphoreType.DMA((2, 3)),
            pltpu.SemaphoreType.DMA((2, 3)),
            pltpu.SemaphoreType.DMA((ITERS, N)),
            pltpu.SemaphoreType.DMA((ITERS, N)),
        ],
        compiler_params=pltpu.CompilerParams(
            collective_id=0, has_side_effects=True, vmem_limit_bytes=60 * 1024 * 1024
        ),
    )(embeddings.T, labels.reshape(1, IMGS), weights, strength.reshape(1, 1))
    return new_weights, losses.reshape(IMGS)


def general(embeddings, labels, weights, strength):
    lam = 16.0 * 0.01 * jnp.exp2(strength[0].astype(jnp.float32))
    full_x = lax.all_gather(embeddings, "cls", axis=1, tiled=True)
    cls_width = weights.shape[1]
    first_class = lax.axis_index("cls") * cls_width
    classes = first_class + lax.iota(jnp.int32, cls_width)
    onehot = (labels[:, None] == classes[None, :]).astype(jnp.float32)
    master = lax.all_gather(weights, "img", axis=0, tiled=True)
    operand = master.astype(jnp.bfloat16)
    losses = jnp.zeros((labels.shape[0],), jnp.float32)
    for step in range(ITERS):
        logits = jnp.dot(full_x, operand, preferred_element_type=jnp.float32) * SCALE
        local_top = jnp.max(logits, axis=1)
        label_term = jnp.sum(logits * onehot, axis=1)
        top = lax.pmax(local_top, "cls")
        total, picked = lax.psum(
            (jnp.sum(jnp.exp(logits - top[:, None]), axis=1), label_term), "cls"
        )
        lse = top + jnp.log(total)
        losses = lse - picked
        resid = (jnp.exp(logits - lse[:, None]) - onehot).astype(jnp.bfloat16)
        grad_local = (
            lax.dot_general(
                full_x, resid, (((0,), (0,)), ((), ())), preferred_element_type=jnp.float32
            )
            * SCALE
        )
        grad = lax.psum(grad_local, "img")
        master = shrink(master, grad, lam)
        operand = master.astype(jnp.bfloat16)
    rows = weights.shape[0]
    new_weights = lax.dynamic_slice_in_dim(master, lax.axis_index("img") * rows, rows, 0)
    return (new_weights, losses)


def solution(mesh):
    placed = (P(("grp", "img"), "cls"), P(("grp", "img")), P(("grp", "img"), "cls"), P("grp"))
    return jax.shard_map(
        fused if mesh.shape["cls"] == N else general,
        mesh=mesh,
        in_specs=placed,
        out_specs=(P(("grp", "img"), "cls"), P(("grp", "img"))),
        check_vma=False,
    )
```

```python
import functools
import math

import jax
import jax.numpy as jnp
from jax import lax
from jax.experimental import pallas as pl
from jax.experimental.pallas import tpu as pltpu
from jax.sharding import PartitionSpec as P

D = 1536
ITERS = 2
MESH = pl.DeviceIdType.MESH
SCALE = 1.0 / math.sqrt(D)

NX, NZ = 2, 4
N = NX * NZ
IMGS, WIDTH, CLS = 1024, 192, 128
UP, DOWN, ACROSS = 0, 1, 2
PARTS = ((0, 96), (96, 64), (160, 32))
LAST = len(PARTS) - 1
CHUNK = 256


def shrink(master, grad, lam):
    moved = master - 16.0 * grad
    return jnp.sign(moved) * jnp.maximum(jnp.abs(moved) - lam, 0.0)


def kernel(x_hbm, lab_ref, w_hbm, s_ref, out_ref, loss_ref,
           w_ref, load, xd, wb, wb2, acc, ex, resid, gsend, grecv, lses, picks,
           send_sem, recv_sem, w_send, w_recv, g_send, g_recv, l_send, l_recv):
    me = lax.axis_index("cls")
    img = lax.axis_index("img")
    grp = lax.axis_index("grp")
    z, x = me // NX, me % NX
    mate = (grp, me, 1 - img)
    has_up, has_down = z < NZ - 1, z > 0
    yes = z >= 0

    def rows(at, n):
        return pl.ds(pl.multiple_of(at, 16), n)

    loads = [
        pltpu.make_async_copy(x_hbm, xd.at[rows(me * WIDTH, WIDTH)], load.at[0]),
        pltpu.make_async_copy(w_hbm, w_ref, load.at[1]),
    ]
    for c in loads:
        c.start()
    barrier = pltpu.get_barrier_semaphore()
    pl.semaphore_signal(barrier, inc=1, device_id=mate, device_id_type=MESH)
    pl.semaphore_signal(
        barrier, inc=1, device_id=(grp, z * NX + 1 - x, img), device_id_type=MESH)

    @pl.when(has_up)
    def _():
        pl.semaphore_signal(barrier, inc=1, device_id=(grp, me + NX, img), device_id_type=MESH)

    @pl.when(has_down)
    def _():
        pl.semaphore_signal(barrier, inc=1, device_id=(grp, me - NX, img), device_id_type=MESH)

    def place(sz, sx, q):
        at, n = PARTS[q]
        return xd.at[rows((sz * NX + sx) * WIDTH + at, n)]

    def copy(sz, sx, q, way):
        to = {UP: me + NX, DOWN: me - NX, ACROSS: z * NX + 1 - x}[way]
        ref = place(sz, sx, q)
        return pltpu.make_async_remote_copy(
            src_ref=ref,
            dst_ref=ref,
            send_sem=send_sem.at[way, sz * NX + sx, q],
            recv_sem=recv_sem.at[sz * NX + sx, q],
            device_id=(grp, to, img),
            device_id_type=MESH,
        )

    started = []

    def send(cond, *args):
        @pl.when(cond)
        def _():
            copy(*args).start()
        started.append((cond, args))

    def arrived(sz, sx, q):
        copy(sz, sx, q, ACROSS).wait_recv()

    def put_weights(buf, values):
        for j in range(2):
            buf[img * 2 + j] = values[384 * j:384 * j + 384].T.astype(jnp.bfloat16)

    loads[1].wait()
    put_weights(wb, w_ref[...])
    acc[...] = jnp.zeros_like(acc)
    loads[0].wait()
    pl.semaphore_wait(barrier, 2 + has_up.astype(jnp.int32) + has_down.astype(jnp.int32))
    send(yes, z, x, LAST, ACROSS)
    for q in range(LAST):
        send(has_up, z, x, q, UP)
        send(has_down, z, x, q, DOWN)
        send(yes, z, x, q, ACROSS)

    def weights_copy(buf, step):
        half = buf.at[pl.ds(img * 2, 2)]
        return pltpu.make_async_remote_copy(
            src_ref=half, dst_ref=half, send_sem=w_send.at[step], recv_sem=w_recv.at[step],
            device_id=mate, device_id_type=MESH)

    def weights_arrived(buf, step):
        half = buf.at[pl.ds((1 - img) * 2, 2)]
        pltpu.make_async_remote_copy(
            src_ref=half, dst_ref=half, send_sem=w_send.at[step], recv_sem=w_recv.at[step],
            device_id=mate, device_id_type=MESH).wait_recv()

    weights_copy(wb, 0).start()

    def add_group(sz):
        for n in range(0, IMGS, CHUNK):
            r = slice(n, n + CHUNK)
            acc[:, r] += jnp.dot(
                wb[sz], xd[rows(sz * 384, 384), r], preferred_element_type=jnp.float32)

    def half_logits(h, r):
        w = jnp.concatenate([wb2[2 * h], wb2[2 * h + 1]], axis=1)
        return jnp.dot(w, xd[rows(h * 768, 768), r], preferred_element_type=jnp.float32)

    def finish(sz):
        for q in range(LAST):
            arrived(sz, 1 - x, q)
        add_group(sz)

    def sides(d):
        return (
            (z - d, z >= d, UP, has_up),
            (z + d, z + d < NZ, DOWN, has_down),
        )

    for d in range(NZ):
        if d > 0:
            for q in range(LAST):
                for sz, here, way, onward in sides(d):
                    @pl.when(here)
                    def _(sz=sz, q=q):
                        arrived(sz, x, q)
                    send(jnp.logical_and(here, onward), sz, x, q, way)
                    send(here, sz, x, q, ACROSS)
        else:
            arrived(z, 1 - x, LAST)
        for sx in (x, 1 - x):
            send(jnp.logical_and(z == d, has_up), z, sx, LAST, UP)
            send(jnp.logical_and(NZ - 1 - z == d, has_down), z, sx, LAST, DOWN)
        if d == 1:
            weights_arrived(wb, 0)
            finish(z)
    for d in range(1, NZ):
        for sz, here, way, onward in sides(d):
            for sx in (x, 1 - x):
                @pl.when(here)
                def _(sz=sz, sx=sx):
                    arrived(sz, sx, LAST)
                send(jnp.logical_and(here, onward), sz, sx, LAST, way)
        for sz, here, _, _ in sides(d - 1) if d > 1 else ():
            @pl.when(here)
            def _(sz=sz):
                finish(sz)

    for sz, here, _, _ in sides(NZ - 1):
        @pl.when(here)
        def _(sz=sz):
            finish(sz)

    lam = 0.16 * jnp.exp2(s_ref[...].astype(jnp.float32))
    first = me * CLS

    def stat_copy(buf, sems, k):
        return pltpu.make_async_remote_copy(
            src_ref=buf.at[me], dst_ref=buf.at[me],
            send_sem=l_send.at[sems, k], recv_sem=l_recv.at[sems, me],
            device_id=(grp, (me + k) % N, img), device_id_type=MESH)

    def stat_arrived(buf, sems, k):
        frm = (me + k) % N
        pltpu.make_async_remote_copy(
            src_ref=buf.at[frm], dst_ref=buf.at[frm],
            send_sem=l_send.at[sems, k], recv_sem=l_recv.at[sems, frm],
            device_id=(grp, frm, img), device_id_type=MESH).wait_recv()

    def grad_copy(step, j):
        return pltpu.make_async_remote_copy(
            src_ref=gsend.at[step, j], dst_ref=grecv.at[step, j],
            send_sem=g_send.at[step, j], recv_sem=g_recv.at[step, j],
            device_id=mate, device_id_type=MESH)

    def grad_part(h, j):
        return lax.dot_general(
            xd[rows(h * 768 + j * 256, 256), :], resid[...], (((1,), (1,)), ((), ())),
            preferred_element_type=jnp.float32)

    for step in range(ITERS):
        last = step == ITERS - 1
        tops = []
        lse_buf = (lses, picks)[step]
        if step > 0:
            weights_arrived(wb2, 1)
        for n in range(0, IMGS, CHUNK):
            r = slice(n, n + CHUNK)
            logits = acc[:, r] * SCALE
            if step > 0:
                logits = (acc[:, r] + half_logits(1 - img, r)) * SCALE
            top = jnp.max(logits, axis=0, keepdims=True)
            e = jnp.exp(logits - top)
            ex[:, r] = e
            lse_buf[me, 0:1, r] = top + jnp.log(jnp.sum(e, axis=0, keepdims=True))
            tops.append(top)
            if last:
                hot = lab_ref[:, r] == first + lax.broadcasted_iota(jnp.int32, (CLS, CHUNK), 0)
                picks[me, 1:2, r] = jnp.sum(jnp.where(hot, logits, 0.0), axis=0, keepdims=True)
        for k in range(1, N):
            stat_copy(lse_buf, step, k).start()
        for k in range(1, N):
            stat_arrived(lse_buf, step, k)
        for n in range(0, IMGS, CHUNK):
            r = slice(n, n + CHUNK)
            parts = [lse_buf[k, 0:1, r] for k in range(N)]
            top = functools.reduce(jnp.maximum, parts)
            lse = top + jnp.log(sum(jnp.exp(p - top) for p in parts))
            if last:
                loss = lse - sum(picks[k, 1:2, r] for k in range(N))
                for i in range(0, CHUNK, 128):
                    row = (n + i) // 128
                    loss_ref[row:row + 1, :] = loss[:, i:i + 128]
            hot = lab_ref[:, r] == first + lax.broadcasted_iota(jnp.int32, (CLS, CHUNK), 0)
            prob = ex[:, r] * jnp.exp(tops[n // CHUNK] - lse)
            resid[:, r] = (prob - jnp.where(hot, 1.0, 0.0)).astype(jnp.bfloat16)
        for j in range(3):
            gsend[step, j] = grad_part(1 - img, j)
            grad_copy(step, j).start()
        for j in range(3):
            r = slice(256 * j, 256 * j + 256)
            grad = grad_part(img, j)
            grad_copy(step, j).wait_recv()
            moved = w_ref[r] - 16.0 * ((grad + grecv[step, j]) * SCALE)
            new = moved - jnp.clip(moved, -lam, lam)
            if last:
                out_ref[r] = new
            else:
                w_ref[r] = new
        if not last:
            put_weights(wb2, w_ref[...])
            weights_copy(wb2, 1).start()
            for n in range(0, IMGS, CHUNK):
                acc[:, n:n + CHUNK] = half_logits(img, slice(n, n + CHUNK))

    for cond, args in started:
        @pl.when(cond)
        def _(args=args):
            copy(*args).wait_send()
    weights_copy(wb, 0).wait_send()
    weights_copy(wb2, 1).wait_send()
    for step in range(ITERS):
        for j in range(3):
            grad_copy(step, j).wait_send()
        for k in range(1, N):
            stat_copy((lses, picks)[step], step, k).wait_send()


def fused(embeddings, labels, weights, strength):
    vmem = pl.BlockSpec(memory_space=pltpu.VMEM)
    hbm = pl.BlockSpec(memory_space=pl.ANY)
    f32, bf16 = jnp.float32, jnp.bfloat16
    new_weights, losses = pl.pallas_call(
        kernel,
        out_shape=(
            jax.ShapeDtypeStruct((768, CLS), f32),
            jax.ShapeDtypeStruct((IMGS // 128, 128), f32),
        ),
        in_specs=[hbm, vmem, hbm, vmem],
        out_specs=(vmem, vmem),
        scratch_shapes=[
            pltpu.VMEM((768, CLS), f32),
            pltpu.SemaphoreType.DMA((2,)),
            pltpu.VMEM((D, IMGS), bf16),
            pltpu.VMEM((4, CLS, 384), bf16),
            pltpu.VMEM((4, CLS, 384), bf16),
            pltpu.VMEM((CLS, IMGS), f32),
            pltpu.VMEM((CLS, IMGS), f32),
            pltpu.VMEM((CLS, IMGS), bf16),
            pltpu.VMEM((ITERS, 3, 256, CLS), f32),
            pltpu.VMEM((ITERS, 3, 256, CLS), f32),
            pltpu.VMEM((N, 1, IMGS), f32),
            pltpu.VMEM((N, 2, IMGS), f32),
            pltpu.SemaphoreType.DMA((3, N, len(PARTS))),
            pltpu.SemaphoreType.DMA((N, len(PARTS))),
            pltpu.SemaphoreType.DMA((2,)),
            pltpu.SemaphoreType.DMA((2,)),
            pltpu.SemaphoreType.DMA((2, 3)),
            pltpu.SemaphoreType.DMA((2, 3)),
            pltpu.SemaphoreType.DMA((ITERS, N)),
            pltpu.SemaphoreType.DMA((ITERS, N)),
        ],
        compiler_params=pltpu.CompilerParams(
            collective_id=0, has_side_effects=True, vmem_limit_bytes=60 * 1024 * 1024
        ),
    )(embeddings.T, labels.reshape(1, IMGS), weights, strength.reshape(1, 1))
    return new_weights, losses.reshape(IMGS)


def general(embeddings, labels, weights, strength):
    lam = 16.0 * 0.01 * jnp.exp2(strength[0].astype(jnp.float32))
    full_x = lax.all_gather(embeddings, "cls", axis=1, tiled=True)
    cls_width = weights.shape[1]
    first_class = lax.axis_index("cls") * cls_width
    classes = first_class + lax.iota(jnp.int32, cls_width)
    onehot = (labels[:, None] == classes[None, :]).astype(jnp.float32)
    master = lax.all_gather(weights, "img", axis=0, tiled=True)
    operand = master.astype(jnp.bfloat16)
    losses = jnp.zeros((labels.shape[0],), jnp.float32)
    for step in range(ITERS):
        logits = jnp.dot(full_x, operand, preferred_element_type=jnp.float32) * SCALE
        local_top = jnp.max(logits, axis=1)
        label_term = jnp.sum(logits * onehot, axis=1)
        top = lax.pmax(local_top, "cls")
        total, picked = lax.psum(
            (jnp.sum(jnp.exp(logits - top[:, None]), axis=1), label_term), "cls"
        )
        lse = top + jnp.log(total)
        losses = lse - picked
        resid = (jnp.exp(logits - lse[:, None]) - onehot).astype(jnp.bfloat16)
        grad_local = (
            lax.dot_general(
                full_x, resid, (((0,), (0,)), ((), ())), preferred_element_type=jnp.float32
            )
            * SCALE
        )
        grad = lax.psum(grad_local, "img")
        master = shrink(master, grad, lam)
        operand = master.astype(jnp.bfloat16)
    rows = weights.shape[0]
    new_weights = lax.dynamic_slice_in_dim(master, lax.axis_index("img") * rows, rows, 0)
    return (new_weights, losses)


def solution(mesh):
    placed = (P(("grp", "img"), "cls"), P(("grp", "img")), P(("grp", "img"), "cls"), P("grp"))
    return jax.shard_map(
        fused if mesh.shape["cls"] == N else general,
        mesh=mesh,
        in_specs=placed,
        out_specs=(P(("grp", "img"), "cls"), P(("grp", "img"))),
        check_vma=False,
    )
```
